32 devices in a mesh: grp: 4 (over y, core), py: 4 (over z), pz: 2 (over x).
Axes of the slice: x: 2, y: 2, z: 4, core: 2. Of those that a mesh axis runs over, the one named last changes fastest.
Arguments:
- velocity: float32 [3, 192, 64, 256], P(None, 'grp', 'py', 'pz'), may hold values from -6 to 6
- spectral_weight: float32 [32, 32, 32, 2, 32, 32], P('py', 'pz', None, None, 'grp'), may hold values from -24 to 24
- lift_weight: float32 [3, 32], replicated, may hold values from -3.5 to 3.5
- mixing_weight: float32 [32, 32], replicated, may hold values from -1 to 1
- project_weight: float32 [32, 3], replicated, may hold values from -1 to 1
Outputs:
- velocity_next: float32 [3, 192, 64, 256], P(None, 'grp', 'py', 'pz')
- grad_spectral: float32 [32, 32, 32, 2, 32, 32], P('py', 'pz', None, None, 'grp')
- grad_mixing: float32 [32, 32], replicated
- mean_loss: float32 [], replicated
The draws below stay inside these ranges and needn't reach their ends.
All inputs are finite; a program needn't handle non-finite values.
Results may differ from the reference program's by a relative error of at most 0.006.
Values may be sent and summed in bfloat16 or wider, within the bound.
No kernel may reach another device: no remote copies, remote signals or barrier semaphores. Data moves between devices by JAX's collectives and lax.ppermute only.
A program may use at most 576 MiB of HBM per device.

```python
import math
import jax
import jax.numpy as jnp
from jax import lax

CX = 48
C = 32
MX = 32
MY = 32
MZ = 32
NX = 192
NY = 64
NZ = 256
N_GRP = 4


def levels(key, dims, pieces, smallest, largest):
    level = 1.0
    for axis_at, blocks in pieces:
        heights = jax.random.uniform(jax.random.fold_in(jax.random.fold_in(key, 6), axis_at), (blocks,), jnp.float32, smallest / len(pieces), largest / len(pieces))
        level = level * jnp.repeat(jnp.exp(heights), dims[axis_at] // blocks).reshape((-1,) + (1,) * (len(dims) - 1 - axis_at))
    return level


def bell_draw(own_key, dims, scale, reach, split=(), kind=jnp.bfloat16):
    values = scale * jax.random.normal(own_key, dims, jnp.float32)
    if split:
        values = values * levels(own_key, dims, split, -0.22, 0.18)
    return jnp.clip(values, -reach, reach).astype(kind)


def setup_inputs(seed: int = 0) -> dict:
    key_of = jax.random.split(jax.random.key(seed), 6)
    velocity = bell_draw(key_of[0], (3, NX, NY, NZ), 1.0, 6.0, ((1, 4), (2, 4), (3, 2)), jnp.float32)
    spectral_weight = bell_draw(key_of[1], (MX, MY, MZ, 2, C, C), 4.0, 24.0, ((0, 4), (1, 2), (4, 4)), jnp.float32)
    lift_weight = bell_draw(key_of[2], (3, C), 3 ** -0.5, 3.5, (), jnp.float32)
    mixing_weight = bell_draw(key_of[3], (C, C), C ** -0.5, 1.0, (), jnp.float32)
    project_weight = bell_draw(key_of[4], (C, 3), C ** -0.5, 1.0, (), jnp.float32)
    return dict(velocity=velocity, spectral_weight=spectral_weight, lift_weight=lift_weight, mixing_weight=mixing_weight, project_weight=project_weight)


time_step = 0.1
viscosity = 0.6
precise = lax.Precision.HIGHEST


def contract(form, left, right):
    return jnp.einsum(form, left.astype(jnp.float32), right.astype(jnp.float32), precision=precise)


def tables(length, mode_count, signed):
    points = jnp.arange(length, dtype=jnp.int32)
    frequency = jnp.arange(mode_count, dtype=jnp.int32)
    if signed:
        frequency = jnp.where(frequency < mode_count // 2, frequency, frequency - mode_count)
    phase_index = (frequency[:, None] * points[None, :]) % length
    angles = phase_index.astype(jnp.float32) * (2.0 * math.pi / length)
    return jnp.cos(angles), jnp.sin(angles)


def forward_x(field_value):
    cosine_table, sine_table = tables(field_value.shape[1], MX, False)
    real_part = contract("cxyz,kx->ckyz", field_value, cosine_table)
    imag_part = -contract("cxyz,kx->ckyz", field_value, sine_table)
    return jnp.stack([real_part, imag_part])


def forward_y(spectrum):
    values = spectrum.astype(jnp.float32)
    cosine_table, sine_table = tables(values.shape[3], MY, True)
    real_part = contract("cmyz,ky->cmkz", values[0], cosine_table) + contract("cmyz,ky->cmkz", values[1], sine_table)
    imag_part = contract("cmyz,ky->cmkz", values[1], cosine_table) - contract("cmyz,ky->cmkz", values[0], sine_table)
    return jnp.stack([real_part, imag_part])


def forward_z(spectrum):
    values = spectrum.astype(jnp.float32)
    cosine_table, sine_table = tables(values.shape[4], MZ, True)
    real_part = contract("cmkz,jz->cmkj", values[0], cosine_table) + contract("cmkz,jz->cmkj", values[1], sine_table)
    imag_part = contract("cmkz,jz->cmkj", values[1], cosine_table) - contract("cmkz,jz->cmkj", values[0], sine_table)
    return jnp.stack([real_part, imag_part])


def inverse_z(spectrum, length):
    values = spectrum.astype(jnp.float32)
    cosine_table, sine_table = tables(length, MZ, True)
    real_part = (contract("cmkj,jz->cmkz", values[0], cosine_table) - contract("cmkj,jz->cmkz", values[1], sine_table)) / length
    imag_part = (contract("cmkj,jz->cmkz", values[1], cosine_table) + contract("cmkj,jz->cmkz", values[0], sine_table)) / length
    return jnp.stack([real_part, imag_part])


def inverse_y(spectrum, length):
    values = spectrum.astype(jnp.float32)
    cosine_table, sine_table = tables(length, MY, True)
    real_part = (contract("cmkz,ky->cmyz", values[0], cosine_table) - contract("cmkz,ky->cmyz", values[1], sine_table)) / length
    imag_part = (contract("cmkz,ky->cmyz", values[1], cosine_table) + contract("cmkz,ky->cmyz", values[0], sine_table)) / length
    return jnp.stack([real_part, imag_part])


def inverse_x(spectrum, length):
    values = spectrum.astype(jnp.float32)
    cosine_table, sine_table = tables(length, MX, False)
    doubling = jnp.where(jnp.arange(MX, dtype=jnp.int32) == 0, 1.0, 2.0).astype(jnp.float32)[:, None]
    return (contract("ckyz,kx->cxyz", values[0], cosine_table * doubling) - contract("ckyz,kx->cxyz", values[1], sine_table * doubling)) / length


def mix_modes(spectrum, weights):
    real_part = contract("cabk,abkco->oabk", spectrum[0], weights[:, :, :, 0]) - contract("cabk,abkco->oabk", spectrum[1], weights[:, :, :, 1])
    imag_part = contract("cabk,abkco->oabk", spectrum[0], weights[:, :, :, 1]) + contract("cabk,abkco->oabk", spectrum[1], weights[:, :, :, 0])
    return jnp.stack([real_part, imag_part])


def grad_modes(spectrum, back_modes):
    real_part = contract("cabk,oabk->abkco", spectrum[0], back_modes[0]) + contract("cabk,oabk->abkco", spectrum[1], back_modes[1])
    imag_part = contract("cabk,oabk->abkco", spectrum[0], back_modes[1]) - contract("cabk,oabk->abkco", spectrum[1], back_modes[0])
    return jnp.stack([real_part, imag_part], axis=3)


def tendency(padded):
    center = padded[:, 1:-1, 1:-1, 1:-1]
    shifted_up = (padded[:, 2:, 1:-1, 1:-1], padded[:, 1:-1, 2:, 1:-1], padded[:, 1:-1, 1:-1, 2:])
    shifted_down = (padded[:, :-2, 1:-1, 1:-1], padded[:, 1:-1, :-2, 1:-1], padded[:, 1:-1, 1:-1, :-2])
    advection = center[0:1] * (shifted_up[0] - shifted_down[0]) + center[1:2] * (shifted_up[1] - shifted_down[1]) + center[2:3] * (shifted_up[2] - shifted_down[2])
    laplacian = shifted_up[0] + shifted_down[0] + shifted_up[1] + shifted_down[1] + shifted_up[2] + shifted_down[2] - 6.0 * center
    return -0.5 * advection + viscosity * laplacian


def coarsen(field_value):
    shape_now = field_value.shape
    blocks = field_value.reshape(shape_now[0], shape_now[1] // 2, 2, shape_now[2] // 2, 2, shape_now[3] // 2, 2)
    return jnp.mean(blocks, axis=(2, 4, 6))


def reference(velocity, spectral_weight, lift_weight, mixing_weight, project_weight):
    flow_cells = (N_GRP - 1) * CX
    domain = velocity[:, :flow_cells]

    def advance(current, anchor, keep_share, step_share):
        padded = jnp.pad(current, ((0, 0), (1, 1), (1, 1), (1, 1)))
        return keep_share * anchor + step_share * (current + time_step * tendency(padded))

    section_one = advance(domain, domain, 0.0, 1.0)
    section_two = advance(section_one, domain, 0.75, 0.25)
    section_three = advance(section_two, domain, 1.0 / 3.0, 2.0 / 3.0)
    velocity_next = jnp.concatenate([section_three, velocity[:, flow_cells:]], axis=1)
    before = coarsen(domain)
    target = coarsen(section_three)
    extent = flow_cells // 2
    height_cells = NY // 2
    depth_cells = NZ // 2
    cell_count = extent * height_cells * depth_cells
    lifted = contract("ic,ixyz->cxyz", lift_weight, before)
    spectrum = forward_z(forward_y(forward_x(lifted)))
    mixed = lax.optimization_barrier(mix_modes(spectrum, spectral_weight).astype(jnp.bfloat16))
    inner_z = lax.optimization_barrier(inverse_z(mixed, depth_cells).astype(jnp.bfloat16))
    inner_y = lax.optimization_barrier(inverse_y(inner_z, height_cells).astype(jnp.bfloat16))
    pre_activation = inverse_x(inner_y, extent) + contract("co,cxyz->oxyz", mixing_weight, lifted)
    sigmoid_gate = jax.nn.sigmoid(pre_activation)
    hidden = pre_activation * sigmoid_gate
    residual = before + contract("ci,cxyz->ixyz", project_weight, hidden) - target
    mean_loss = 0.5 * jnp.sum(residual * residual) / cell_count
    grad_pre = contract("ci,ixyz->cxyz", project_weight, residual) * sigmoid_gate * (1.0 + pre_activation * (1.0 - sigmoid_gate))
    grad_mixing = contract("cxyz,oxyz->co", lifted, grad_pre) / cell_count
    back_x = lax.optimization_barrier(forward_x(grad_pre).astype(jnp.bfloat16))
    back_y = lax.optimization_barrier(forward_y(back_x).astype(jnp.bfloat16))
    wave_index = jnp.arange(MX, dtype=jnp.int32)
    factor = jnp.where(wave_index == 0, 1.0, 2.0).astype(jnp.float32) / cell_count
    back_modes = forward_z(back_y) * factor[None, None, :, None, None]
    grad_spectral = grad_modes(spectrum, back_modes)
    return velocity_next, grad_spectral, grad_mixing, mean_loss
```

```python
import math

import jax
import jax.numpy as jnp
import numpy as np
from jax import lax
from jax.experimental import pallas as pl
from jax.experimental.pallas import tpu as pltpu
from jax.sharding import PartitionSpec as P

MX = 32
MY = 32
MZ = 32


time_step = 0.1
viscosity = 0.6
precise = lax.Precision.HIGHEST


def with_halo(cells, sides, width):
    for axis, dim in sides:
        count = lax.axis_size(axis)
        ends = count - 1
        head = lax.slice_in_dim(cells, 0, width, axis=dim)
        tail = lax.slice_in_dim(cells, cells.shape[dim] - width, cells.shape[dim], axis=dim)
        cells = jnp.concatenate(
            [
                lax.ppermute(tail, axis, [(i, (i + 1) % count) for i in range(ends)]),
                cells,
                lax.ppermute(head, axis, [((i + 1) % count, i) for i in range(ends)]),
            ],
            axis=dim,
        )
    return cells


def contract(form, left, right):
    return jnp.einsum(form, left, right, precision=precise)


def tables(length, mode_count, signed):
    points = jnp.arange(length, dtype=jnp.int32)
    frequency = jnp.arange(mode_count, dtype=jnp.int32)
    if signed:
        frequency = jnp.where(frequency < mode_count // 2, frequency, frequency - mode_count)
    phase_index = frequency[:, None] * points[None, :] % length
    angles = phase_index.astype(jnp.float32) * (2.0 * math.pi / length)
    return (jnp.cos(angles), jnp.sin(angles))


def forward_x(field_value):
    cosine_table, sine_table = tables(field_value.shape[1], MX, False)
    real_part = contract("cxyz,kx->ckyz", field_value, cosine_table)
    imag_part = -contract("cxyz,kx->ckyz", field_value, sine_table)
    return jnp.stack([real_part, imag_part])


def forward_y(spectrum):
    values = spectrum.astype(jnp.float32)
    cosine_table, sine_table = tables(values.shape[3], MY, True)
    real_part = contract("cmyz,ky->cmkz", values[0], cosine_table) + contract(
        "cmyz,ky->cmkz", values[1], sine_table
    )
    imag_part = contract("cmyz,ky->cmkz", values[1], cosine_table) - contract(
        "cmyz,ky->cmkz", values[0], sine_table
    )
    return jnp.stack([real_part, imag_part])


def forward_z(spectrum):
    values = spectrum.astype(jnp.float32)
    cosine_table, sine_table = tables(values.shape[4], MZ, True)
    real_part = contract("cmkz,jz->cmkj", values[0], cosine_table) + contract(
        "cmkz,jz->cmkj", values[1], sine_table
    )
    imag_part = contract("cmkz,jz->cmkj", values[1], cosine_table) - contract(
        "cmkz,jz->cmkj", values[0], sine_table
    )
    return jnp.stack([real_part, imag_part])


def inverse_z(spectrum, length):
    values = spectrum.astype(jnp.float32)
    cosine_table, sine_table = tables(length, MZ, True)
    real_part = (
        contract("cmkj,jz->cmkz", values[0], cosine_table)
        - contract("cmkj,jz->cmkz", values[1], sine_table)
    ) / length
    imag_part = (
        contract("cmkj,jz->cmkz", values[1], cosine_table)
        + contract("cmkj,jz->cmkz", values[0], sine_table)
    ) / length
    return jnp.stack([real_part, imag_part])


def inverse_y(spectrum, length):
    values = spectrum.astype(jnp.float32)
    cosine_table, sine_table = tables(length, MY, True)
    real_part = (
        contract("cmkz,ky->cmyz", values[0], cosine_table)
        - contract("cmkz,ky->cmyz", values[1], sine_table)
    ) / length
    imag_part = (
        contract("cmkz,ky->cmyz", values[1], cosine_table)
        + contract("cmkz,ky->cmyz", values[0], sine_table)
    ) / length
    return jnp.stack([real_part, imag_part])


def inverse_x(spectrum, length):
    values = spectrum.astype(jnp.float32)
    cosine_table, sine_table = tables(length, MX, False)
    doubling = jnp.where(jnp.arange(MX, dtype=jnp.int32) == 0, 1.0, 2.0).astype(jnp.float32)[
        :, None
    ]
    return (
        contract("ckyz,kx->cxyz", values[0], cosine_table * doubling)
        - contract("ckyz,kx->cxyz", values[1], sine_table * doubling)
    ) / length


def mix_modes(spectrum, weights):
    real_part = contract("cabk,abkco->oabk", spectrum[0], weights[:, :, :, 0]) - contract(
        "cabk,abkco->oabk", spectrum[1], weights[:, :, :, 1]
    )
    imag_part = contract("cabk,abkco->oabk", spectrum[0], weights[:, :, :, 1]) + contract(
        "cabk,abkco->oabk", spectrum[1], weights[:, :, :, 0]
    )
    return jnp.stack([real_part, imag_part])


def grad_modes(spectrum, back_modes):
    real_part = contract("cabk,oabk->abkco", spectrum[0], back_modes[0]) + contract(
        "cabk,oabk->abkco", spectrum[1], back_modes[1]
    )
    imag_part = contract("cabk,oabk->abkco", spectrum[0], back_modes[1]) - contract(
        "cabk,oabk->abkco", spectrum[1], back_modes[0]
    )
    return jnp.stack([real_part, imag_part], axis=3)


def tendency(padded):
    center = padded[:, 1:-1, 1:-1, 1:-1]
    shifted_up = (padded[:, 2:, 1:-1, 1:-1], padded[:, 1:-1, 2:, 1:-1], padded[:, 1:-1, 1:-1, 2:])
    shifted_down = (
        padded[:, :-2, 1:-1, 1:-1],
        padded[:, 1:-1, :-2, 1:-1],
        padded[:, 1:-1, 1:-1, :-2],
    )
    advection = (
        center[0:1] * (shifted_up[0] - shifted_down[0])
        + center[1:2] * (shifted_up[1] - shifted_down[1])
        + center[2:3] * (shifted_up[2] - shifted_down[2])
    )
    laplacian = (
        shifted_up[0]
        + shifted_down[0]
        + shifted_up[1]
        + shifted_down[1]
        + shifted_up[2]
        + shifted_down[2]
        - 6.0 * center
    )
    return -0.5 * advection + viscosity * laplacian


def coarsen(field_value):
    shape_now = field_value.shape
    blocks = field_value.reshape(
        shape_now[0], shape_now[1] // 2, 2, shape_now[2] // 2, 2, shape_now[3] // 2, 2
    )
    return jnp.mean(blocks, axis=(2, 4, 6))


def general(velocity, spectral_weight, lift_weight, mixing_weight, project_weight):
    groups = lax.axis_size("grp")
    trainer = lax.axis_index("grp") == groups - 1

    def on_trainer(function, operand):
        return lax.cond(
            trainer,
            function,
            lambda operand_value: jax.tree.map(jnp.zeros_like, function(operand_value)),
            operand,
        )

    def opening(snapshot):
        return forward_x(contract("ic,ixyz->cxyz", lift_weight, snapshot))

    weights_full = lax.all_gather(spectral_weight, "grp", axis=4, tiled=True)
    field_start = jnp.where(trainer, jnp.zeros_like(velocity), velocity)
    first_coarse = coarsen(field_start)

    def advance(current, anchor, keep_share, step_share):
        padded = with_halo(
            current.astype(jnp.bfloat16), (("grp", 1), ("py", 2), ("pz", 3)), 1
        ).astype(current.dtype)

        def update(operands):
            padded_value, current_value = operands
            return keep_share * anchor + step_share * (
                current_value + time_step * tendency(padded_value)
            )

        return lax.cond(
            trainer, lambda operands: jnp.zeros_like(operands[1]), update, (padded, current)
        )

    section_one = advance(field_start, field_start, 0.0, 1.0)
    section_two = advance(section_one, field_start, 0.75, 0.25)
    section_three = advance(section_two, field_start, 1.0 / 3.0, 2.0 / 3.0)
    velocity_next = jnp.where(trainer, velocity, section_three)
    second_coarse = coarsen(section_three)
    first_all, second_all = (
        lax.all_gather(first_coarse, "grp", axis=1, tiled=True),
        lax.all_gather(second_coarse, "grp", axis=1, tiled=True),
    )
    extent = (groups - 1) * first_coarse.shape[1]
    before = first_all[:, :extent]
    target = second_all[:, :extent]
    height_cells = first_coarse.shape[2] * lax.axis_size("py")
    depth_cells = first_coarse.shape[3] * lax.axis_size("pz")
    cell_count = extent * height_cells * depth_cells
    spectrum_x = on_trainer(opening, before)
    spectrum_x = lax.all_to_all(spectrum_x, "py", split_axis=2, concat_axis=3, tiled=True)
    spectrum_y = on_trainer(forward_y, spectrum_x)
    spectrum_y = lax.all_to_all(spectrum_y, "pz", split_axis=3, concat_axis=4, tiled=True)
    spectrum = on_trainer(lambda values: forward_z(values), spectrum_y)

    def middle(operands):
        values, weights = operands
        mixed_modes = mix_modes(values, weights).astype(jnp.bfloat16)
        return inverse_z(mixed_modes, depth_cells).astype(jnp.bfloat16)

    inner_z = on_trainer(middle, (spectrum, weights_full))
    inner_z = lax.all_to_all(inner_z, "pz", split_axis=4, concat_axis=3, tiled=True)
    inner_y = on_trainer(
        lambda values: inverse_y(values, height_cells).astype(jnp.bfloat16), inner_z
    )
    inner_y = lax.all_to_all(inner_y, "py", split_axis=3, concat_axis=2, tiled=True)

    def opening_close(operands):
        values, before_value = operands
        lifted = contract("ic,ixyz->cxyz", lift_weight, before_value)
        pre_activation = inverse_x(values, extent) + contract(
            "co,cxyz->oxyz", mixing_weight, lifted
        )
        sigmoid_gate = jax.nn.sigmoid(pre_activation)
        hidden = pre_activation * sigmoid_gate
        projected = contract("ci,cxyz->ixyz", project_weight, hidden)
        return (lifted, pre_activation, sigmoid_gate, projected)

    lifted, pre_activation, sigmoid_gate, projected = on_trainer(opening_close, (inner_y, before))

    def closing(operands):
        lifted_value, pre_value, gate_value, projected_value, before_value, target_value = operands
        residual = before_value + projected_value - target_value
        grad_pre = (
            contract("ci,ixyz->cxyz", project_weight, residual)
            * gate_value
            * (1.0 + pre_value * (1.0 - gate_value))
        )
        mix_part = contract("cxyz,oxyz->co", lifted_value, grad_pre)
        loss_term = 0.5 * jnp.sum(residual * residual)
        return (forward_x(grad_pre).astype(jnp.bfloat16), mix_part, loss_term)

    back_x, mix_term, loss_term = on_trainer(
        closing, (lifted, pre_activation, sigmoid_gate, projected, before, target)
    )
    back_x = lax.all_to_all(back_x, "py", split_axis=2, concat_axis=3, tiled=True)
    back_y = on_trainer(lambda values: forward_y(values).astype(jnp.bfloat16), back_x)
    back_y = lax.all_to_all(back_y, "pz", split_axis=3, concat_axis=4, tiled=True)
    local_modes = spectrum.shape[2]
    wave_index = lax.axis_index("py") * local_modes + jnp.arange(local_modes, dtype=jnp.int32)
    factor = jnp.where(wave_index == 0, 1.0, 2.0).astype(jnp.float32) / cell_count
    back_modes = on_trainer(
        lambda values: forward_z(values) * factor[None, None, :, None, None], back_y
    )
    grad_term = on_trainer(
        lambda operands: grad_modes(operands[0], operands[1]), (spectrum, back_modes)
    )
    grad_spectral = lax.psum_scatter(
        grad_term.astype(jnp.bfloat16), "grp", scatter_dimension=4, tiled=True
    ).astype(jnp.float32)
    mix_total, loss_total = lax.psum((mix_term, loss_term), ("grp", "py", "pz"))
    return (velocity_next, grad_spectral, mix_total / cell_count, loss_total / cell_count)


ALL = ("grp", "py", "pz")
C = 32
LANES = 128
VMEM = 60 * 1024 * 1024


def dot(left, right, dims=((1,), (0,))):
    return lax.dot_general(
        left, right, (dims, ((), ())), precision=precise, preferred_element_type=jnp.float32
    )


def dot16(left, right, dims=((1,), (0,))):
    return lax.dot_general(
        left.astype(jnp.bfloat16),
        right.astype(jnp.bfloat16),
        (dims, ((), ())),
        preferred_element_type=jnp.float32,
    )


def call(kernel, out_shape, scratch=(), **kwargs):
    return pl.pallas_call(
        kernel,
        out_shape=out_shape,
        scratch_shapes=list(scratch),
        compiler_params=pltpu.CompilerParams(vmem_limit_bytes=VMEM),
        **kwargs,
    )


def shape_of(*dims, kind=jnp.float32):
    return jax.ShapeDtypeStruct(dims, kind)


def signed(count):
    index = np.arange(count)
    return np.where(index < count // 2, index, index - count)


def turn(frequency, point, length):
    angle = 2.0 * np.pi * ((frequency * point) % length) / length
    return np.cos(angle), np.sin(angle)


class Plan:
    def __init__(self, groups, rows, cols, cells):
        self.G, self.PY, self.PZ = groups, rows, cols
        self.cells = cells
        self.nx, self.ny, self.nz = cells
        self.cx, self.cy, self.cz = (n // 2 for n in cells)
        self.X = (groups - 1) * self.cx
        self.Y = self.cy * rows
        self.Z = self.cz * cols
        self.D = groups * rows * cols
        self.W = rows * cols
        self.a = MX // rows
        self.b = MY // cols
        self.kz = MZ // self.W
        self.no = C // groups
        self.ky = 4
        self.t = self.b // self.ky
        self.XP = -(-self.X // 16) * 16
        self.Q = self.XP * self.no // LANES
        self.count = self.X * self.Y * self.Z

    def tables(self):
        f32 = np.float32
        G, PY, PZ, D, W = self.G, self.PY, self.PZ, self.D, self.W
        kx = np.arange(MX)
        fy, fz = signed(MY), signed(MZ)
        out = {}
        c, s = turn(kx[:, None], np.arange(self.X)[None, :], self.X)
        out["xm"] = np.concatenate([c, -s], 0).astype(f32)
        tz = np.zeros((PZ, 2, 2, LANES, LANES))
        for p in range(PZ):
            z = p * self.cz + np.arange(self.cz)
            c, s = turn(fz[None, :], z[:, None], self.Z)
            for h in range(2):
                for k, v in enumerate((c, s)):
                    tz[p, k, h, h * self.cz : (h + 1) * self.cz] = np.tile(v, (1, self.ky))
        out["tz"] = tz.astype(f32)
        tiles = MY // self.ky
        cy = np.zeros((PY, 2, tiles * self.cy, LANES))
        for p in range(PY):
            y = p * self.cy + np.arange(self.cy)
            c, s = turn(fy[:, None], y[None, :], self.Y)
            for k, v in enumerate((c, s)):
                v = v.reshape(tiles, self.ky, self.cy).transpose(0, 2, 1)
                cy[p, k] = np.repeat(v, MZ, axis=2).reshape(tiles * self.cy, LANES)
        out["cy"] = cy.astype(f32)
        d = np.arange(D)
        g, py, pz = d // W, (d // PZ) % PY, d % PZ
        yrow = py * self.cy + g * PZ + pz
        ky_of = np.arange(MY).reshape(PZ, self.t, self.ky)
        c, s = turn(fy[None, :], yrow[:, None], self.Y)
        eye = np.eye(self.kz)

        def block(rr, ri, ir, ii):
            m = np.zeros((D, 2, self.kz, PZ, self.t, 2, self.ky, self.kz))
            for i, row in enumerate(((rr, ri), (ir, ii))):
                for o, v in enumerate(row):
                    v = v[:, ky_of]
                    m[:, o, :, :, :, i] = np.einsum("dpty,kl->dkptyl", v, eye)
            n = D * 2 * self.kz
            return m.reshape(n, PZ * LANES)

        out["m1"] = block(c, s, -s, c).astype(f32)
        out["m2"] = block(-s, c, -c, -s).astype(f32)

        def back(rr, ri, ir, ii):
            m = np.zeros((D, 2, self.kz, PZ, self.t, 2, self.ky, self.kz))
            for i, row in enumerate(((rr, ri), (ir, ii))):
                for o, v in enumerate(row):
                    v = v[:, ky_of]
                    m[:, i, :, :, :, o] = np.einsum("dpty,kl->dkptyl", v, eye)
            return m.reshape(D * 2 * self.kz, PZ * LANES)

        out["n1"] = back(c, -s, s, c).astype(f32)
        out["n2"] = back(-s, -c, c, -s).astype(f32)
        weight = np.where(kx == 0, 1.0, 2.0)
        c, s = turn(kx[:, None], np.arange(self.X)[None, :], self.X)
        eye = np.eye(self.no)

        def wide(v):
            m = np.zeros((MX, self.no, self.XP, self.no))
            m[:, :, : self.X] = np.einsum("kx,op->koxp", v, eye)
            return m.reshape(MX * self.no, self.XP * self.no).astype(f32)

        inverse = weight[:, None] / self.X
        forward = weight[:, None] / self.count
        out["cx"], out["sx"] = wide(c * inverse), wide(s * inverse)
        out["cxt"], out["sxt"] = wide(c * forward), wide(s * forward)
        c, s = turn(fz[:, None], np.arange(self.Z)[None, :], self.Z)

        def zrows(first, second, scale):
            v = np.stack([first, second]).reshape(2, W, self.kz, self.Z).transpose(1, 0, 2, 3)
            return (v * scale).reshape(W * 2 * self.kz, self.Z).astype(f32)

        out["zi"] = zrows(c, -s, 1.0 / (self.Y * self.Z))
        out["zf"] = zrows(c, -s, 1.0)
        pairs = np.zeros((2, LANES, LANES))
        for h in range(2):
            z = np.arange(LANES)
            pairs[h, z, h * self.cz + z // 2] = 0.125
        out["pairs"] = pairs.astype(f32)
        return out


def coarse_rows(ref, plan, row):
    total = None
    for dx in range(2):
        for dy in range(2):
            start = dx * plan.ny + 2 * row + dy
            part = ref[pl.ds(start, 3 * plan.cx, stride=2 * plan.ny), :]
            total = part if total is None else total + part
    return total


def put_faces(ref, plan, xlo, xhi):
    n = plan.ny
    for i in range(3):
        base = i * plan.nx * n
        xlo[i * n : (i + 1) * n, :] = ref[base : base + n, :]
        xhi[i * n : (i + 1) * n, :] = ref[base + (plan.nx - 1) * n : base + plan.nx * n, :]


def lane_ids(rows):
    return lax.broadcasted_iota(jnp.int32, (rows, LANES), 1)


def put_z(plane, i, x, plan, zlo, zhi):
    n = plan.ny
    rows = slice(i * n, (i + 1) * n)
    here = lane_ids(n) == x
    zlo[rows, :] = jnp.where(here, pltpu.roll(plane, x, 1), zlo[rows, :])
    zhi[rows, :] = jnp.where(here, pltpu.roll(plane, x + 1, 1), zhi[rows, :])


def opening_kernel(plan, u, pairs, coarse, xlo, xhi, ylo, yhi, zlo, zhi):
    count = 3 * plan.nx
    ylo[...] = u[pl.ds(0, count, stride=plan.ny), :]
    yhi[...] = u[pl.ds(plan.ny - 1, count, stride=plan.ny), :]
    put_faces(u, plan, xlo, xhi)
    for q in range(plan.cy // 2):
        total = dot(coarse_rows(u, plan, 2 * q), pairs[0]) + dot(
            coarse_rows(u, plan, 2 * q + 1), pairs[1]
        )
        coarse[:, q * LANES : (q + 1) * LANES] = total
    zlo[...] = jnp.zeros_like(zlo)
    zhi[...] = jnp.zeros_like(zhi)

    def body(step, carry):
        for k in range(4):
            x = step * 4 + k
            for i in range(3):
                start = pl.multiple_of((i * plan.nx + x) * plan.ny, plan.ny)
                put_z(u[pl.ds(start, plan.ny), :], i, x, plan, zlo, zhi)
        return carry

    lax.fori_loop(0, plan.nx // 4, body, 0)


def stage_kernel(plan, keep, share, last, *refs):
    if last:
        flag, u, anchor, hxlo, hxhi, hylo, hyhi, hzlo, hzhi, pairs, out, both, hold = refs
    else:
        u, anchor, hxlo, hxhi, hylo, hyhi, hzlo, hzhi, out, xlo, xhi, ylo, yhi, zlo, zhi = refs
        zlo[...] = jnp.zeros_like(zlo)
        zhi[...] = jnp.zeros_like(zhi)
    n = plan.ny
    lanes = lane_ids(n)
    rows = lax.broadcasted_iota(jnp.int32, (n, LANES), 0)

    def plane_of(ref, i, x):
        return ref[pl.ds(pl.multiple_of((i * plan.nx + x) * n, n), n), :]

    def one(x):
        center = [plane_of(u, i, x) for i in range(3)]
        for i in range(3):
            c = center[i]
            r = i * plan.nx + x
            face = slice(i * n, (i + 1) * n)
            down = jnp.where(x == 0, hxlo[face, :], plane_of(u, i, jnp.maximum(x - 1, 0)))
            up = jnp.where(
                x == plan.nx - 1, hxhi[face, :], plane_of(u, i, jnp.minimum(x + 1, plan.nx - 1))
            )
            ydown = jnp.where(rows == 0, hylo[pl.ds(r, 1), :], pltpu.roll(c, 1, 0))
            yup = jnp.where(rows == n - 1, hyhi[pl.ds(r, 1), :], pltpu.roll(c, n - 1, 0))
            zdown = jnp.where(
                lanes == 0, pltpu.roll(hzlo[face, :], LANES - x, 1), pltpu.roll(c, 1, 1)
            )
            zup = jnp.where(
                lanes == LANES - 1,
                pltpu.roll(hzhi[face, :], LANES - 1 - x, 1),
                pltpu.roll(c, LANES - 1, 1),
            )
            advection = (
                center[0] * (up - down) + center[1] * (yup - ydown) + center[2] * (zup - zdown)
            )
            laplacian = up + down + yup + ydown + zup + zdown - 6.0 * c
            new = share * (c + time_step * (viscosity * laplacian - 0.5 * advection))
            if keep:
                new = new + keep * plane_of(anchor, i, x)
            out[pl.ds(pl.multiple_of(r * n, n), n), :] = new
            if not last:
                ylo[pl.ds(r, 1), :] = new[0:1]
                yhi[pl.ds(r, 1), :] = new[n - 1 : n]
                put_z(new, i, x, plan, zlo, zhi)

    def body(step, carry):
        for k in range(4):
            one(step * 4 + k)
        return carry

    lax.fori_loop(0, plan.nx // 4, body, 0)
    if last:
        for row in range(plan.cy):
            first = coarse_rows(anchor, plan, row)
            gap = first - coarse_rows(out, plan, row)
            hold[row] = dot(first, pairs[0]) + dot(gap, pairs[1])
        both[...] = hold[...].astype(jnp.bfloat16)

        @pl.when(flag[0] > 0)
        def _():
            out[...] = anchor[...]
    else:
        put_faces(out, plan, xlo, xhi)


def spectrum_kernel(plan, cg, xm, tz, cy, hold):
    tiles = MY // plan.ky
    for i in range(3):
        field = jnp.concatenate(
            [cg[g, i * plan.cx : (i + 1) * plan.cx, :] for g in range(plan.G - 1)], axis=0
        )
        f = dot(xm[...], field)
        real, imag = [], []
        for y in range(plan.cy):
            part = f[:, (y // 2) * LANES : (y // 2 + 1) * LANES]
            cosine, sine = dot(part, tz[0, y % 2]), dot(part, tz[1, y % 2])
            real.append(cosine[:MX] + sine[MX:])
            imag.append(cosine[MX:] - sine[:MX])
        for t in range(tiles):
            sum_re = sum_im = 0.0
            for y in range(plan.cy):
                row = t * plan.cy + y
                c, s = cy[0, row : row + 1, :], cy[1, row : row + 1, :]
                sum_re = sum_re + c * real[y] + s * imag[y]
                sum_im = sum_im + c * imag[y] - s * real[y]
            owner, inner = t // plan.t, t % plan.t
            for p in range(plan.PY):
                rows = slice(p * plan.a, (p + 1) * plan.a)
                for k, value in enumerate((sum_re, sum_im)):
                    at = ((i * 2 + k) * plan.t + inner) * plan.a
                    hold[p * plan.PZ + owner, at : at + plan.a, :] = value[rows]


def halves(value):
    high = value.astype(jnp.bfloat16)
    return high, (value - high.astype(jnp.float32)).astype(jnp.bfloat16)


def mode_block(plan, rows_ref, w, t, a):
    n = plan.ky * plan.kz
    lanes = lax.broadcasted_iota(jnp.int32, (n, n * 2 * plan.no), 1) // (2 * plan.no)
    here = lanes == lax.broadcasted_iota(jnp.int32, (n, n * 2 * plan.no), 0)
    parts = [
        jnp.where(here, rows_ref[w, k, pl.ds(t * plan.a + a, 1), :], 0.0) for k in range(2)
    ]
    return jnp.concatenate(parts, axis=0)


def mix_kernel(plan, received, coef, weights, rows_out, out, hold):
    a = pl.program_id(0)
    n = plan.ky * plan.kz
    wide = n * 2 * plan.no

    @pl.when(a == 0)
    def _():
        total = received[0]
        for source in range(1, plan.W):
            total = total + received[source]
        high, low = halves(total)
        lane_in = lax.broadcasted_iota(jnp.int32, (LANES, wide), 0)
        mode = lax.broadcasted_iota(jnp.int32, (LANES, wide), 1) // (2 * plan.no)
        step = plan.t * plan.a
        for w in range(plan.W):
            want = (mode // plan.kz) * MZ + w * plan.kz + mode % plan.kz
            pick = jnp.where(lane_in == want, 1.0, 0.0).astype(jnp.bfloat16)
            spread = dot16(high, pick) + dot16(low, pick)
            for k in range(2):
                rows = 0.0
                for j in range(6):
                    at = k * 6 + j
                    rows = rows + coef[at : at + 1, :] * spread[j * step : (j + 1) * step]
                rows_out[w, k] = rows

    at = pl.multiple_of(a * plan.no, plan.no)
    for w in range(plan.W):
        parts = []
        for t in range(plan.t):
            block = weights[
                0, t * plan.ky : (t + 1) * plan.ky, w * plan.kz : (w + 1) * plan.kz
            ].reshape(wide, C)
            high, low = halves(mode_block(plan, rows_out, w, t, a))
            weight, rest = halves(block)
            both = dot16(jnp.concatenate([high, low], axis=0), weight)
            parts.append(both[: 2 * n] + both[2 * n :] + dot16(high, rest))
        mixed = jnp.concatenate(parts, axis=0).T
        for g in range(plan.G):
            hold[g * plan.W + w, pl.ds(at, plan.no), :] = mixed[g * plan.no : (g + 1) * plan.no]

    @pl.when(a == plan.a - 1)
    def _():
        out[...] = hold[...].astype(jnp.bfloat16)


def inverse_kernel(plan, received, m1, m2, cx, sx, out, hold):
    rows = []
    for p in range(plan.PY):
        cols = []
        for q in range(plan.PZ):
            total = 0.0
            for g in range(plan.G):
                total = total + received[g * plan.W + p * plan.PZ + q].astype(jnp.float32)
            cols.append(total)
        rows.append(jnp.concatenate(cols, axis=1))
    modes = jnp.concatenate(rows, axis=0)
    nt = ((1,), (1,))
    value = dot(dot(m1[...], modes, nt), cx[...]) + dot(dot(m2[...], modes, nt), sx[...])
    for q in range(plan.Q):
        hold[:, q * 8 : (q + 1) * 8, :] = value[:, q * LANES : (q + 1) * LANES].reshape(
            plan.D, 8, LANES
        )
    out[...] = hold[...].astype(jnp.bfloat16)


def point_kernel(plan, received, both, zi, zf, mixc, projc, out, taken, hold):
    W, G, no = plan.W, plan.G, plan.no
    per = LANES // no
    taken[...] = received[...].astype(jnp.float32)
    tn, nt = ((0,), (0,)), ((1,), (1,))
    moments = [[0.0] * 3 for _ in range(G)]
    loss = 0.0
    for q in range(plan.Q):
        x = slice(q * per, (q + 1) * per)
        before = [both[0, i, x] for i in range(3)]
        gap = [both[1, i, x] for i in range(3)]
        pres, gates = [], []
        shown = [0.0] * 3
        for g in range(G):
            modes = taken[g * W : (g + 1) * W, q * 8 : (q + 1) * 8, :].reshape(W * 8, LANES)
            pre = dot(modes, zi[...], tn).reshape(per, no, LANES)
            for i in range(3):
                pre = pre + mixc[g * 3 + i] * before[i]
            gate = jax.nn.sigmoid(pre)
            hidden = pre * gate
            for i in range(3):
                shown[i] = shown[i] + jnp.sum(projc[g * 3 + i] * hidden, axis=1, keepdims=True)
            pres.append(pre)
            gates.append(gate)
        residual = [shown[i] + gap[i] for i in range(3)]
        loss = loss + sum(jnp.sum(r * r, axis=0) for r in residual)
        for g in range(G):
            slope = sum(projc[g * 3 + i] * residual[i] for i in range(3))
            slope = slope * gates[g] * (1.0 + pres[g] * (1.0 - gates[g]))
            for i in range(3):
                moments[g][i] = moments[g][i] + jnp.sum(slope * before[i], axis=0)
            modes = dot(zf[...], slope.reshape(LANES, LANES), nt)
            hold[g * W : (g + 1) * W, q * 8 : (q + 1) * 8, :] = modes.reshape(W, 8, LANES)
    lanes = lane_ids(no)
    tile = jnp.zeros((no, LANES), jnp.float32)

    def place(tile, value, index):
        high = value.astype(jnp.bfloat16).astype(jnp.float32)
        tile = jnp.where(lanes == index, high, tile)
        return jnp.where(lanes == index + LANES // 2, value - high, tile)

    for g in range(G):
        for i in range(3):
            tile = place(tile, jnp.sum(moments[g][i], axis=1, keepdims=True), g * 3 + i)
    tile = place(tile, jnp.broadcast_to(jnp.sum(loss, axis=1, keepdims=True), (no, 1)), G * 3)
    hold[:, plan.Q * 8 :, :] = jnp.broadcast_to(tile[None], (plan.D, no, LANES))
    out[...] = hold[...].astype(jnp.bfloat16)


def forward_kernel(plan, received, cxt, sxt, n1, n2, out, stats, taken):
    taken[...] = received[...].astype(jnp.float32)
    stats[...] = jnp.sum(taken[:, plan.Q * 8 :, :], axis=0)
    first = second = 0.0
    nt = ((1,), (1,))
    for q in range(plan.Q):
        rows = taken[:, q * 8 : (q + 1) * 8, :].reshape(plan.D * 8, LANES)
        cols = slice(q * LANES, (q + 1) * LANES)
        first = first + dot(cxt[:, cols], rows, nt)
        second = second + dot(sxt[:, cols], rows, nt)
    modes = (dot(first, n1[...]) + dot(second, n2[...])).astype(jnp.bfloat16)
    size = plan.a * plan.no
    for p in range(plan.PY):
        for q in range(plan.PZ):
            tile = modes[p * size : (p + 1) * size, q * LANES : (q + 1) * LANES]
            for g in range(plan.G):
                out[g * plan.W + p * plan.PZ + q] = tile


def grad_kernel(plan, rows_ref, received, out, taken):
    a = pl.program_id(0)
    n = plan.ky * plan.kz

    @pl.when(a == 0)
    def _():
        taken[...] = received[...].astype(jnp.float32)

    at = pl.multiple_of(a * plan.no, plan.no)
    for w in range(plan.W):
        back = jnp.concatenate(
            [taken[g * plan.W + w, pl.ds(at, plan.no), :] for g in range(plan.G)], axis=0
        ).T
        for t in range(plan.t):
            block = dot16(
                mode_block(plan, rows_ref, w, t, a), back[t * 2 * n : (t + 1) * 2 * n], ((0,), (0,))
            )
            out[0, t * plan.ky : (t + 1) * plan.ky, w * plan.kz : (w + 1) * plan.kz] = (
                block.reshape(plan.ky, plan.kz, 2, plan.no, C)
            )


def halos(faces, plan):
    xlo, xhi, ylo, yhi, zlo, zhi = faces
    out = []
    for low, high, axis, count in (
        (xlo, xhi, "grp", plan.G - 1),
        (ylo, yhi, "py", plan.PY),
        (zlo, zhi, "pz", plan.PZ),
    ):
        up = [(i, i + 1) for i in range(count - 1)]
        out.append(lax.ppermute(high, axis, up))
        out.append(lax.ppermute(low, axis, [(j, i) for i, j in up]))
    return out


def everyone(plan, velocity, spectral_weight, lift_weight, mixing_weight, project_weight):
    tables = plan.tables()
    G, W, D = plan.G, plan.W, plan.D
    n = plan.ny
    group = lax.axis_index("grp")
    flag = (group == G - 1).astype(jnp.int32)[None]
    cells = 3 * plan.nx * n
    field = velocity.reshape(cells, LANES)
    faces_shape = [shape_of(3 * n, LANES)] * 2 + [shape_of(3 * plan.nx, LANES)] * 2
    faces_shape = faces_shape + [shape_of(3 * n, LANES)] * 2
    full = shape_of(cells, LANES)

    def bind(kernel, *args):
        return lambda *refs: kernel(plan, *args, *refs)

    coarse, *faces = call(
        bind(opening_kernel), [shape_of(3 * plan.cx, plan.cy * plan.cz)] + faces_shape
    )(field, tables["pairs"])
    edges = halos(faces, plan)

    gathered = lax.all_gather(coarse, "grp", axis=0)
    tz = lax.dynamic_index_in_dim(jnp.asarray(tables["tz"]), lax.axis_index("pz"), 0, False)
    cy = lax.dynamic_index_in_dim(jnp.asarray(tables["cy"]), lax.axis_index("py"), 0, False)
    lines = 6 * plan.t * plan.a
    spectra = call(
        bind(spectrum_kernel),
        shape_of(W, lines, LANES),
    )(gathered, tables["xm"], tz, cy)
    spectra = lax.all_to_all(spectra, ("py", "pz"), 0, 0, tiled=True)

    lift = lax.dynamic_slice_in_dim(lift_weight, group * plan.no, plan.no, axis=1)
    zero = jnp.zeros_like(lift)
    first = jnp.concatenate([lift, zero], axis=1)
    second = jnp.concatenate([zero, lift], axis=1)
    coef = jnp.stack(
        [jnp.stack([first, -second], 1), jnp.stack([second, first], 1)]
    ).reshape(12, 2 * plan.no)
    wide = plan.ky * plan.kz * 2 * plan.no
    coef = jnp.tile(coef, (1, plan.ky * plan.kz))
    lift_rows, mixed = pl.pallas_call(
        bind(mix_kernel),
        grid=(plan.a,),
        in_specs=[
            pl.BlockSpec((W, lines, LANES), lambda i: (0, 0, 0)),
            pl.BlockSpec((12, wide), lambda i: (0, 0)),
            pl.BlockSpec((1, plan.b, MZ, 2, plan.no, C), lambda i: (i, 0, 0, 0, 0, 0)),
        ],
        out_specs=[
            pl.BlockSpec((W, 2, plan.t * plan.a, wide), lambda i: (0, 0, 0, 0)),
            pl.BlockSpec((D, plan.a * plan.no, LANES), lambda i: (0, 0, 0)),
        ],
        out_shape=[
            shape_of(W, 2, plan.t * plan.a, wide),
            shape_of(D, plan.a * plan.no, LANES, kind=jnp.bfloat16),
        ],
        scratch_shapes=[pltpu.VMEM((D, plan.a * plan.no, LANES), jnp.float32)],
        compiler_params=pltpu.CompilerParams(vmem_limit_bytes=VMEM),
    )(spectra, coef, spectral_weight)
    mixed = lax.all_to_all(mixed, ALL, 0, 0, tiled=True)

    tall = plan.Q * 8
    inner = call(
        bind(inverse_kernel),
        shape_of(D, tall, LANES, kind=jnp.bfloat16),
        [pltpu.VMEM((D, tall, LANES), jnp.float32)],
    )(mixed, tables["m1"], tables["m2"], tables["cx"], tables["sx"])
    inner = lax.all_to_all(inner, ALL, 0, 0, tiled=True)

    one, *faces = call(bind(stage_kernel, 0.0, 1.0, False), [full] + faces_shape)(
        field, field, *edges
    )
    edges = halos(faces, plan)
    two, *faces = call(bind(stage_kernel, 0.75, 0.25, False), [full] + faces_shape)(
        one, field, *edges
    )
    edges = halos(faces, plan)
    both_shape = (plan.cy, 3 * plan.cx, LANES)
    smem = pl.BlockSpec(memory_space=pltpu.SMEM)
    vmem = pl.BlockSpec(memory_space=pltpu.VMEM)
    three, both = call(
        bind(stage_kernel, 1.0 / 3.0, 2.0 / 3.0, True),
        [full, shape_of(*both_shape, kind=jnp.bfloat16)],
        [pltpu.VMEM(both_shape, jnp.float32)],
        in_specs=[smem] + [vmem] * 9,
    )(flag, two, field, *edges, tables["pairs"])
    velocity_next = three.reshape(velocity.shape)

    both = lax.all_to_all(both, ("grp", "pz"), 0, 0, tiled=True)
    both = both.reshape(G, plan.PZ, 3, plan.cx, 2, plan.cz)[: G - 1].astype(jnp.float32)
    both = both.transpose(4, 2, 0, 3, 1, 5).reshape(2, 3, plan.X, plan.Z)
    both = jnp.pad(both, ((0, 0), (0, 0), (0, plan.XP - plan.X), (0, 0)))[:, :, :, None, :]

    def column(value):
        value = value.reshape(3, G, plan.no).transpose(1, 0, 2).reshape(G * 3, plan.no, 1)
        return jnp.broadcast_to(value, (G * 3, plan.no, LANES))

    mixc = column(contract("ic,co->io", lift_weight, mixing_weight))
    projc = column(project_weight.T)
    back = call(
        bind(point_kernel),
        shape_of(D, tall + 8, LANES, kind=jnp.bfloat16),
        [pltpu.VMEM((D, tall, LANES), jnp.float32), pltpu.VMEM((D, tall + 8, LANES), jnp.float32)],
    )(inner, both, tables["zi"], tables["zf"], mixc, projc)
    back = lax.all_to_all(back, ALL, 0, 0, tiled=True)

    modes, stats = call(
        bind(forward_kernel),
        [shape_of(D, plan.a * plan.no, LANES, kind=jnp.bfloat16), shape_of(plan.no, LANES)],
        [pltpu.VMEM((D, tall + 8, LANES), jnp.float32)],
    )(back, tables["cxt"], tables["sxt"], tables["n1"], tables["n2"])
    modes = lax.all_to_all(modes, ALL, 0, 0, tiled=True)

    grad_spectral = pl.pallas_call(
        bind(grad_kernel),
        grid=(plan.a,),
        in_specs=[
            pl.BlockSpec((W, 2, plan.t * plan.a, wide), lambda i: (0, 0, 0, 0)),
            pl.BlockSpec((D, plan.a * plan.no, LANES), lambda i: (0, 0, 0)),
        ],
        out_specs=pl.BlockSpec((1, plan.b, MZ, 2, plan.no, C), lambda i: (i, 0, 0, 0, 0, 0)),
        out_shape=shape_of(*spectral_weight.shape),
        scratch_shapes=[pltpu.VMEM((D, plan.a * plan.no, LANES), jnp.float32)],
        compiler_params=pltpu.CompilerParams(vmem_limit_bytes=VMEM),
    )(lift_rows, modes)

    half = LANES // 2
    stats = (stats[:, :half] + stats[:, half:]) / plan.count
    moments = stats[:, : G * 3].reshape(plan.no, G, 3).transpose(2, 1, 0).reshape(3, C)
    grad_mixing = contract("ic,io->co", lift_weight, moments)
    return velocity_next, grad_spectral, grad_mixing, 0.5 * stats[0, G * 3]


def plan_of(mesh, velocity):
    groups, rows, cols = (mesh.shape[name] for name in ALL)
    plan = Plan(groups, rows, cols, velocity.shape[1:])
    fits = (
        plan.nz == LANES
        and plan.Z == LANES
        and plan.W * plan.kz == MZ
        and plan.kz * 2 == 8
        and plan.no == 8
        and plan.ky * MZ == LANES
        and plan.t * plan.ky == plan.b
        and plan.t * 2 * plan.ky * plan.kz == LANES
        and plan.cy == groups * cols
        and plan.cx % 8 == 0
        and plan.a % 8 == 0
    )
    return plan if fits else None


def solution(mesh):
    def local(velocity, *weights):
        plan = plan_of(mesh, velocity)
        if plan is None:
            return general(velocity, *weights)
        return everyone(plan, velocity, *weights)

    return jax.shard_map(
        local,
        mesh=mesh,
        in_specs=(
            P(None, "grp", "py", "pz"),
            P("py", "pz", None, None, "grp", None),
            P(),
            P(),
            P(),
        ),
        out_specs=(P(None, "grp", "py", "pz"), P("py", "pz", None, None, "grp", None), P(), P()),
        check_vma=False,
    )
```

```python
import math

import jax
import jax.numpy as jnp
import numpy as np
from jax import lax
from jax.experimental import pallas as pl
from jax.experimental.pallas import tpu as pltpu
from jax.sharding import PartitionSpec as P


MX = 32
MY = 32
MZ = 32


time_step = 0.1
viscosity = 0.6
precise = lax.Precision.HIGHEST


def with_halo(cells, sides, width):
    for axis, dim in sides:
        count = lax.axis_size(axis)
        ends = count - 1
        head = lax.slice_in_dim(cells, 0, width, axis=dim)
        tail = lax.slice_in_dim(cells, cells.shape[dim] - width, cells.shape[dim], axis=dim)
        cells = jnp.concatenate(
            [
                lax.ppermute(tail, axis, [(i, (i + 1) % count) for i in range(ends)]),
                cells,
                lax.ppermute(head, axis, [((i + 1) % count, i) for i in range(ends)]),
            ],
            axis=dim,
        )
    return cells


def contract(form, left, right):
    return jnp.einsum(form, left, right, precision=precise)


def tables(length, mode_count, signed):
    points = jnp.arange(length, dtype=jnp.int32)
    frequency = jnp.arange(mode_count, dtype=jnp.int32)
    if signed:
        frequency = jnp.where(frequency < mode_count // 2, frequency, frequency - mode_count)
    phase_index = frequency[:, None] * points[None, :] % length
    angles = phase_index.astype(jnp.float32) * (2.0 * math.pi / length)
    return (jnp.cos(angles), jnp.sin(angles))


def forward_x(field_value):
    cosine_table, sine_table = tables(field_value.shape[1], MX, False)
    real_part = contract("cxyz,kx->ckyz", field_value, cosine_table)
    imag_part = -contract("cxyz,kx->ckyz", field_value, sine_table)
    return jnp.stack([real_part, imag_part])


def forward_y(spectrum):
    values = spectrum.astype(jnp.float32)
    cosine_table, sine_table = tables(values.shape[3], MY, True)
    real_part = contract("cmyz,ky->cmkz", values[0], cosine_table) + contract(
        "cmyz,ky->cmkz", values[1], sine_table
    )
    imag_part = contract("cmyz,ky->cmkz", values[1], cosine_table) - contract(
        "cmyz,ky->cmkz", values[0], sine_table
    )
    return jnp.stack([real_part, imag_part])


def forward_z(spectrum):
    values = spectrum.astype(jnp.float32)
    cosine_table, sine_table = tables(values.shape[4], MZ, True)
    real_part = contract("cmkz,jz->cmkj", values[0], cosine_table) + contract(
        "cmkz,jz->cmkj", values[1], sine_table
    )
    imag_part = contract("cmkz,jz->cmkj", values[1], cosine_table) - contract(
        "cmkz,jz->cmkj", values[0], sine_table
    )
    return jnp.stack([real_part, imag_part])


def inverse_z(spectrum, length):
    values = spectrum.astype(jnp.float32)
    cosine_table, sine_table = tables(length, MZ, True)
    real_part = (
        contract("cmkj,jz->cmkz", values[0], cosine_table)
        - contract("cmkj,jz->cmkz", values[1], sine_table)
    ) / length
    imag_part = (
        contract("cmkj,jz->cmkz", values[1], cosine_table)
        + contract("cmkj,jz->cmkz", values[0], sine_table)
    ) / length
    return jnp.stack([real_part, imag_part])


def inverse_y(spectrum, length):
    values = spectrum.astype(jnp.float32)
    cosine_table, sine_table = tables(length, MY, True)
    real_part = (
        contract("cmkz,ky->cmyz", values[0], cosine_table)
        - contract("cmkz,ky->cmyz", values[1], sine_table)
    ) / length
    imag_part = (
        contract("cmkz,ky->cmyz", values[1], cosine_table)
        + contract("cmkz,ky->cmyz", values[0], sine_table)
    ) / length
    return jnp.stack([real_part, imag_part])


def inverse_x(spectrum, length):
    values = spectrum.astype(jnp.float32)
    cosine_table, sine_table = tables(length, MX, False)
    doubling = jnp.where(jnp.arange(MX, dtype=jnp.int32) == 0, 1.0, 2.0).astype(jnp.float32)[
        :, None
    ]
    return (
        contract("ckyz,kx->cxyz", values[0], cosine_table * doubling)
        - contract("ckyz,kx->cxyz", values[1], sine_table * doubling)
    ) / length


def mix_modes(spectrum, weights):
    real_part = contract("cabk,abkco->oabk", spectrum[0], weights[:, :, :, 0]) - contract(
        "cabk,abkco->oabk", spectrum[1], weights[:, :, :, 1]
    )
    imag_part = contract("cabk,abkco->oabk", spectrum[0], weights[:, :, :, 1]) + contract(
        "cabk,abkco->oabk", spectrum[1], weights[:, :, :, 0]
    )
    return jnp.stack([real_part, imag_part])


def grad_modes(spectrum, back_modes):
    real_part = contract("cabk,oabk->abkco", spectrum[0], back_modes[0]) + contract(
        "cabk,oabk->abkco", spectrum[1], back_modes[1]
    )
    imag_part = contract("cabk,oabk->abkco", spectrum[0], back_modes[1]) - contract(
        "cabk,oabk->abkco", spectrum[1], back_modes[0]
    )
    return jnp.stack([real_part, imag_part], axis=3)


def tendency(padded):
    center = padded[:, 1:-1, 1:-1, 1:-1]
    shifted_up = (padded[:, 2:, 1:-1, 1:-1], padded[:, 1:-1, 2:, 1:-1], padded[:, 1:-1, 1:-1, 2:])
    shifted_down = (
        padded[:, :-2, 1:-1, 1:-1],
        padded[:, 1:-1, :-2, 1:-1],
        padded[:, 1:-1, 1:-1, :-2],
    )
    advection = (
        center[0:1] * (shifted_up[0] - shifted_down[0])
        + center[1:2] * (shifted_up[1] - shifted_down[1])
        + center[2:3] * (shifted_up[2] - shifted_down[2])
    )
    laplacian = (
        shifted_up[0]
        + shifted_down[0]
        + shifted_up[1]
        + shifted_down[1]
        + shifted_up[2]
        + shifted_down[2]
        - 6.0 * center
    )
    return -0.5 * advection + viscosity * laplacian


def coarsen(field_value):
    shape_now = field_value.shape
    blocks = field_value.reshape(
        shape_now[0], shape_now[1] // 2, 2, shape_now[2] // 2, 2, shape_now[3] // 2, 2
    )
    return jnp.mean(blocks, axis=(2, 4, 6))


def general(velocity, spectral_weight, lift_weight, mixing_weight, project_weight):
    groups = lax.axis_size("grp")
    trainer = lax.axis_index("grp") == groups - 1

    def on_trainer(function, operand):
        return lax.cond(
            trainer,
            function,
            lambda operand_value: jax.tree.map(jnp.zeros_like, function(operand_value)),
            operand,
        )

    def opening(snapshot):
        return forward_x(contract("ic,ixyz->cxyz", lift_weight, snapshot))

    weights_full = lax.all_gather(spectral_weight, "grp", axis=4, tiled=True)
    field_start = jnp.where(trainer, jnp.zeros_like(velocity), velocity)
    first_coarse = coarsen(field_start)

    def advance(current, anchor, keep_share, step_share):
        padded = with_halo(
            current.astype(jnp.bfloat16), (("grp", 1), ("py", 2), ("pz", 3)), 1
        ).astype(current.dtype)

        def update(operands):
            padded_value, current_value = operands
            return keep_share * anchor + step_share * (
                current_value + time_step * tendency(padded_value)
            )

        return lax.cond(
            trainer, lambda operands: jnp.zeros_like(operands[1]), update, (padded, current)
        )

    section_one = advance(field_start, field_start, 0.0, 1.0)
    section_two = advance(section_one, field_start, 0.75, 0.25)
    section_three = advance(section_two, field_start, 1.0 / 3.0, 2.0 / 3.0)
    velocity_next = jnp.where(trainer, velocity, section_three)
    second_coarse = coarsen(section_three)
    first_all, second_all = (
        lax.all_gather(first_coarse, "grp", axis=1, tiled=True),
        lax.all_gather(second_coarse, "grp", axis=1, tiled=True),
    )
    extent = (groups - 1) * first_coarse.shape[1]
    before = first_all[:, :extent]
    target = second_all[:, :extent]
    height_cells = first_coarse.shape[2] * lax.axis_size("py")
    depth_cells = first_coarse.shape[3] * lax.axis_size("pz")
    cell_count = extent * height_cells * depth_cells
    spectrum_x = on_trainer(opening, before)
    spectrum_x = lax.all_to_all(spectrum_x, "py", split_axis=2, concat_axis=3, tiled=True)
    spectrum_y = on_trainer(forward_y, spectrum_x)
    spectrum_y = lax.all_to_all(spectrum_y, "pz", split_axis=3, concat_axis=4, tiled=True)
    spectrum = on_trainer(lambda values: forward_z(values), spectrum_y)

    def middle(operands):
        values, weights = operands
        mixed_modes = mix_modes(values, weights).astype(jnp.bfloat16)
        return inverse_z(mixed_modes, depth_cells).astype(jnp.bfloat16)

    inner_z = on_trainer(middle, (spectrum, weights_full))
    inner_z = lax.all_to_all(inner_z, "pz", split_axis=4, concat_axis=3, tiled=True)
    inner_y = on_trainer(
        lambda values: inverse_y(values, height_cells).astype(jnp.bfloat16), inner_z
    )
    inner_y = lax.all_to_all(inner_y, "py", split_axis=3, concat_axis=2, tiled=True)

    def opening_close(operands):
        values, before_value = operands
        lifted = contract("ic,ixyz->cxyz", lift_weight, before_value)
        pre_activation = inverse_x(values, extent) + contract(
            "co,cxyz->oxyz", mixing_weight, lifted
        )
        sigmoid_gate = jax.nn.sigmoid(pre_activation)
        hidden = pre_activation * sigmoid_gate
        projected = contract("ci,cxyz->ixyz", project_weight, hidden)
        return (lifted, pre_activation, sigmoid_gate, projected)

    lifted, pre_activation, sigmoid_gate, projected = on_trainer(opening_close, (inner_y, before))

    def closing(operands):
        lifted_value, pre_value, gate_value, projected_value, before_value, target_value = operands
        residual = before_value + projected_value - target_value
        grad_pre = (
            contract("ci,ixyz->cxyz", project_weight, residual)
            * gate_value
            * (1.0 + pre_value * (1.0 - gate_value))
        )
        mix_part = contract("cxyz,oxyz->co", lifted_value, grad_pre)
        loss_term = 0.5 * jnp.sum(residual * residual)
        return (forward_x(grad_pre).astype(jnp.bfloat16), mix_part, loss_term)

    back_x, mix_term, loss_term = on_trainer(
        closing, (lifted, pre_activation, sigmoid_gate, projected, before, target)
    )
    back_x = lax.all_to_all(back_x, "py", split_axis=2, concat_axis=3, tiled=True)
    back_y = on_trainer(lambda values: forward_y(values).astype(jnp.bfloat16), back_x)
    back_y = lax.all_to_all(back_y, "pz", split_axis=3, concat_axis=4, tiled=True)
    local_modes = spectrum.shape[2]
    wave_index = lax.axis_index("py") * local_modes + jnp.arange(local_modes, dtype=jnp.int32)
    factor = jnp.where(wave_index == 0, 1.0, 2.0).astype(jnp.float32) / cell_count
    back_modes = on_trainer(
        lambda values: forward_z(values) * factor[None, None, :, None, None], back_y
    )
    grad_term = on_trainer(
        lambda operands: grad_modes(operands[0], operands[1]), (spectrum, back_modes)
    )
    grad_spectral = lax.psum_scatter(
        grad_term.astype(jnp.bfloat16), "grp", scatter_dimension=4, tiled=True
    ).astype(jnp.float32)
    mix_total, loss_total = lax.psum((mix_term, loss_term), ("grp", "py", "pz"))
    return (velocity_next, grad_spectral, mix_total / cell_count, loss_total / cell_count)


ALL = ("grp", "py", "pz")
C = 32
LANES = 128
VMEM = 24 * 1024 * 1024


def dot(left, right, dims=((1,), (0,))):
    return lax.dot_general(
        left, right, (dims, ((), ())), precision=precise, preferred_element_type=jnp.float32
    )


def dot16(left, right, dims=((1,), (0,))):
    return lax.dot_general(
        left.astype(jnp.bfloat16),
        right.astype(jnp.bfloat16),
        (dims, ((), ())),
        preferred_element_type=jnp.float32,
    )


def halves(value):
    high = value.astype(jnp.bfloat16)
    return high, (value - high.astype(jnp.float32)).astype(jnp.bfloat16)


def dot3(left, right, dims=((1,), (0,))):
    return (
        dot16(left[0], right[0], dims)
        + dot16(left[1], right[0], dims)
        + dot16(left[0], right[1], dims)
    )


def call(kernel, out_shape, scratch=(), **kwargs):
    return pl.pallas_call(
        kernel,
        out_shape=out_shape,
        scratch_shapes=list(scratch),
        compiler_params=pltpu.CompilerParams(vmem_limit_bytes=VMEM),
        **kwargs,
    )


def shape_of(*dims, kind=jnp.float32):
    return jax.ShapeDtypeStruct(dims, kind)


def signed(count):
    index = np.arange(count)
    return np.where(index < count // 2, index, index - count)


def turn(frequency, point, length):
    angle = 2.0 * np.pi * ((frequency * point) % length) / length
    return np.cos(angle), np.sin(angle)


def table_halves(value):
    value = np.asarray(value, np.float32)
    high = value.astype(jnp.bfloat16)
    return np.stack([high, (value - high.astype(np.float32)).astype(jnp.bfloat16)])


class Plan:
    def __init__(self, groups, rows, cols, cells):
        self.G, self.PY, self.PZ = groups, rows, cols
        self.nx, self.ny, self.nz = cells
        self.cx, self.cy, self.cz = (n // 2 for n in cells)
        self.X = (groups - 1) * self.cx
        self.Y = self.cy * rows
        self.Z = self.cz * cols
        self.D = groups * rows * cols
        self.W = rows * cols
        self.a = MX // rows
        self.b = MY // cols
        self.kz = MZ // self.W
        self.no = C // groups
        self.ky = 4
        self.t = self.b // self.ky
        self.XP = -(-self.X // 16) * 16
        self.Q = self.XP * self.no // LANES
        self.half = self.cx // 2
        self.pad = -(-self.half // 8) * 8
        self.count = self.X * self.Y * self.Z

    def tables(self):
        f32 = np.float32
        G, PY, PZ, D, W = self.G, self.PY, self.PZ, self.D, self.W
        kx = np.arange(MX)
        fy, fz = signed(MY), signed(MZ)
        out = {}
        xm = np.zeros((2, 2 * MX, G - 1, self.pad))
        for h in range(2):
            x = (np.arange(G - 1)[:, None] * self.cx + 2 * np.arange(self.half) + h)[None]
            c, s = turn(kx[:, None, None], x, self.X)
            xm[h, :, :, : self.half] = np.concatenate([c, -s], 0)
        out["xm"] = xm.reshape(2, 2 * MX, (G - 1) * self.pad).astype(f32)
        tz = np.zeros((PZ, 2, 2, self.cz, 2, 2, MZ))
        for p in range(PZ):
            c, s = turn(fz[None, :], (p * self.cz + np.arange(self.cz))[:, None], self.Z)
            tz[p, 0, :, :, 0, 0], tz[p, 0, :, :, 0, 1] = c, -s
            tz[p, 1, :, :, 0, 0], tz[p, 1, :, :, 0, 1] = s, c
        out["tz"] = tz.reshape(PZ, 2, LANES, LANES).astype(f32)
        d = np.arange(D)
        g, py, pz = d // W, (d // PZ) % PY, d % PZ
        yrow = py * self.cy + g * PZ + pz
        ky_of = np.arange(MY).reshape(PZ, self.t, self.ky)
        c, s = turn(fy[None, :], yrow[:, None], self.Y)
        eye = np.eye(self.kz)
        lane = ky_of[:, :, np.repeat(np.arange(self.ky), MZ)]
        cy = np.stack([v.T[lane].transpose(0, 1, 3, 2) for v in (c, s)], axis=1)
        out["cy"] = cy.reshape(PZ, 2, self.t * D, LANES).astype(f32)

        def block(rr, ri, ir, ii):
            m = np.zeros((D, 2, self.kz, PZ, self.t, 2, self.ky, self.kz))
            for i, row in enumerate(((rr, ri), (ir, ii))):
                for o, v in enumerate(row):
                    v = v[:, ky_of]
                    m[:, o, :, :, :, i] = np.einsum("dpty,kl->dkptyl", v, eye)
            n = D * 2 * self.kz
            return m.reshape(n, PZ * LANES)

        out["m"] = table_halves(
            np.concatenate([block(c, s, -s, c), block(-s, c, -c, -s)], axis=0)
        )

        def back(rr, ri, ir, ii):
            m = np.zeros((D, 2, self.kz, PZ, self.t, 2, self.ky, self.kz))
            for i, row in enumerate(((rr, ri), (ir, ii))):
                for o, v in enumerate(row):
                    v = v[:, ky_of]
                    m[:, i, :, :, :, o] = np.einsum("dpty,kl->dkptyl", v, eye)
            return m.reshape(D * 2 * self.kz, PZ * LANES)

        out["n"] = table_halves(
            np.concatenate([back(c, -s, s, c), back(-s, -c, c, -s)], axis=0)
        )
        weight = np.where(kx == 0, 1.0, 2.0)
        c, s = turn(kx[:, None], np.arange(self.X)[None, :], self.X)
        eye = np.eye(self.no)

        def wide(v):
            m = np.zeros((MX, self.no, self.XP, self.no))
            m[:, :, : self.X] = np.einsum("kx,op->koxp", v, eye)
            return m.reshape(MX * self.no, self.XP * self.no)

        inverse = weight[:, None] / self.X
        forward = weight[:, None] / self.count
        out["ex"] = table_halves(np.concatenate([wide(c * inverse), wide(s * inverse)], 0))
        out["fx"] = table_halves(np.concatenate([wide(c * forward), wide(s * forward)], 0))
        c, s = turn(fz[:, None], np.arange(self.Z)[None, :], self.Z)

        def zrows(first, second, scale):
            v = np.stack([first, second]).reshape(2, W, self.kz, self.Z).transpose(1, 0, 2, 3)
            return table_halves((v * scale).reshape(W * 2 * self.kz, self.Z)).reshape(-1, self.Z)

        out["zi"] = zrows(c, -s, 1.0 / (self.Y * self.Z))
        out["zf"] = zrows(c, -s, 1.0)
        pairs = np.zeros((2, LANES, LANES))
        for h in range(2):
            z = np.arange(LANES)
            pairs[h, z, h * self.cz + z // 2] = 0.125
        out["pairs"] = pairs.astype(jnp.bfloat16)
        return out


def coarse_rows(ref, plan, row, parity):
    total = None
    for dx in range(2):
        for dy in range(2):
            start = (2 * parity + dx) * plan.ny + 2 * row + dy
            part = ref[pl.ds(start, 3 * plan.half, stride=4 * plan.ny), :]
            total = part if total is None else total + part
    return total


def put_coarse(plan, hold, row, even, odd, pairs):
    total = sum(dot16(part, pairs[0]) for part in halves(even))
    total = total + sum(dot16(part, pairs[1]) for part in halves(odd))
    hold[row] = jnp.zeros((3 * plan.pad, LANES), jnp.float32)
    for i in range(3):
        rows = total[i * plan.half : (i + 1) * plan.half]
        hold[row, i * plan.pad : i * plan.pad + plan.half, :] = rows


def put_faces(ref, plan, xlo, xhi):
    n = plan.ny
    for i in range(3):
        base = i * plan.nx * n
        xlo[i * n : (i + 1) * n, :] = ref[base : base + n, :]
        xhi[i * n : (i + 1) * n, :] = ref[base + (plan.nx - 1) * n : base + plan.nx * n, :]


def lane_ids(rows):
    return lax.broadcasted_iota(jnp.int32, (rows, LANES), 1)


def put_z(plane, i, x, col, plan, zface):
    n = plan.ny
    rows = slice(i * n, (i + 1) * n)
    moved = pltpu.roll(plane, x + 1 - col, 1)
    zface[rows, :] = jnp.where(lane_ids(n) == x, moved, zface[rows, :])


def opening_kernel(plan, place, u, pairs, coarse, xlo, xhi, ylo, yhi, zface):
    count = 3 * plan.nx
    col = place[1]
    ylo[...] = u[pl.ds(0, count, stride=plan.ny), :]
    yhi[...] = u[pl.ds(plan.ny - 1, count, stride=plan.ny), :]
    put_faces(u, plan, xlo, xhi)
    for row in range(plan.cy):
        even, odd = (coarse_rows(u, plan, row, h) for h in range(2))
        put_coarse(plan, coarse, row, even, odd, pairs)
    zface[...] = jnp.zeros_like(zface)

    def body(step, carry):
        for k in range(4):
            x = step * 4 + k
            for i in range(3):
                start = pl.multiple_of((i * plan.nx + x) * plan.ny, plan.ny)
                put_z(u[pl.ds(start, plan.ny), :], i, x, col, plan, zface)
        return carry

    lax.fori_loop(0, plan.nx // 4, body, 0)


def stage_kernel(plan, keep, share, last, place, after, *refs):
    if last:
        u, anchor, hxlo, hxhi, hylo, hyhi, hz, pairs, out, gap, hold = refs
    else:
        u, anchor, hxlo, hxhi, hylo, hyhi, hz, out, xlo, xhi, ylo, yhi, zface = refs
        zface[...] = jnp.zeros_like(zface)
    n = plan.ny
    col = place[1]
    lanes = lane_ids(n)
    rows = lax.broadcasted_iota(jnp.int32, (n, LANES), 0)
    zfirst = jnp.where(col == 0, 0.0, 1.0)
    zlast = 1.0 - zfirst

    def plane_of(ref, i, x):
        return ref[pl.ds(pl.multiple_of((i * plan.nx + x) * n, n), n), :]

    def one(x):
        center = [plane_of(u, i, x) for i in range(3)]
        for i in range(3):
            c = center[i]
            r = i * plan.nx + x
            face = slice(i * n, (i + 1) * n)
            down = jnp.where(x == 0, hxlo[face, :], plane_of(u, i, jnp.maximum(x - 1, 0)))
            up = jnp.where(
                x == plan.nx - 1, hxhi[face, :], plane_of(u, i, jnp.minimum(x + 1, plan.nx - 1))
            )
            ydown = jnp.where(rows == 0, hylo[pl.ds(r, 1), :], pltpu.roll(c, 1, 0))
            yup = jnp.where(rows == n - 1, hyhi[pl.ds(r, 1), :], pltpu.roll(c, n - 1, 0))
            edge = pltpu.roll(hz[face, :], LANES - 1 + col - x, 1)
            zdown = jnp.where(lanes == 0, edge * zfirst, pltpu.roll(c, 1, 1))
            zup = jnp.where(lanes == LANES - 1, edge * zlast, pltpu.roll(c, LANES - 1, 1))
            advection = (
                center[0] * (up - down) + center[1] * (yup - ydown) + center[2] * (zup - zdown)
            )
            laplacian = up + down + yup + ydown + zup + zdown - 6.0 * c
            new = share * (c + time_step * (viscosity * laplacian - 0.5 * advection))
            if keep:
                new = new + keep * plane_of(anchor, i, x)
            out[pl.ds(pl.multiple_of(r * n, n), n), :] = new
            if not last:
                ylo[pl.ds(r, 1), :] = new[0:1]
                yhi[pl.ds(r, 1), :] = new[n - 1 : n]
                put_z(new, i, x, col, plan, zface)

    def body(step, carry):
        for k in range(4):
            one(step * 4 + k)
        return carry

    lax.fori_loop(0, plan.nx // 4, body, 0)
    if last:
        for row in range(plan.cy):
            even, odd = (
                coarse_rows(anchor, plan, row, h) - coarse_rows(out, plan, row, h)
                for h in range(2)
            )
            put_coarse(plan, hold, row, even, odd, pairs)
        gap[...] = hold[...].astype(jnp.bfloat16)

        @pl.when(place[0] > 0)
        def _():
            out[...] = anchor[...]
    else:
        put_faces(out, plan, xlo, xhi)


def spectrum_kernel(plan, received, xm, tz, out):
    low = lane_ids(2 * MX) < LANES // 2
    tiles = []
    for i in range(3):
        total = 0.0
        for p in range(plan.PZ):
            rows = slice(i * plan.pad, (i + 1) * plan.pad)
            field = jnp.concatenate(
                [received[g * plan.PZ + p, rows, :] for g in range(plan.G - 1)], axis=0
            )
            f = jnp.where(low, dot(xm[0], field), dot(xm[1], field))
            total = total + dot(f[:MX], tz[p, 0]) + dot(f[MX:], tz[p, 1])
        tiles.append(total)
    tiles = [tiles[0] + pltpu.roll(tiles[1], LANES // 2, 1), tiles[2]]
    for p in range(plan.PY):
        for k in range(2):
            value = tiles[k][p * plan.a : (p + 1) * plan.a]
            for g in range(plan.G):
                for q in range(plan.PZ):
                    at = g * plan.W + p * plan.PZ + q
                    out[at, k * plan.a : (k + 1) * plan.a, :] = value


def gather_modes(plan, received, cy, total):
    a, D = plan.a, plan.D
    slot_of = lane_ids(D * a) // MZ
    spread = []
    for j in range(6):
        rows = received[:, (j // 4) * a : (j // 4 + 1) * a, :].reshape(D * a, LANES)
        rows = jnp.where(slot_of == j % 4, rows, 0.0)
        rows = rows + pltpu.roll(rows, 2 * MZ, 1)
        spread.append(rows + pltpu.roll(rows, MZ, 1))
    for t in range(plan.t):
        sums = [0.0] * 6
        for d in range(D):
            at = t * D + d
            c, s = cy[0, at : at + 1, :], cy[1, at : at + 1, :]
            for i in range(3):
                real = spread[2 * i][d * a : (d + 1) * a]
                imag = spread[2 * i + 1][d * a : (d + 1) * a]
                sums[2 * i] = sums[2 * i] + c * real + s * imag
                sums[2 * i + 1] = sums[2 * i + 1] + c * imag - s * real
        for j in range(6):
            at = (j * plan.t + t) * a
            total[at : at + a, :] = sums[j]


def mode_block(plan, rows_ref, w, t, a):
    n = plan.ky * plan.kz
    lanes = lax.broadcasted_iota(jnp.int32, (n, n * 2 * plan.no), 1) // (2 * plan.no)
    here = lanes == lax.broadcasted_iota(jnp.int32, (n, n * 2 * plan.no), 0)
    parts = [
        jnp.where(here, rows_ref[w, k, pl.ds(t * plan.a + a, 1), :], 0.0) for k in range(2)
    ]
    return jnp.concatenate(parts, axis=0)


def mix_kernel(plan, received, cy, coef, weights, *refs):
    rows_out, out, hold, total = refs[-4:]
    a = pl.program_id(0)
    n = plan.ky * plan.kz
    wide = n * 2 * plan.no

    @pl.when(a == 0)
    def _():
        gather_modes(plan, received, cy, total)
        high, low = halves(total[...])
        lane_in = lax.broadcasted_iota(jnp.int32, (LANES, wide), 0)
        mode = lax.broadcasted_iota(jnp.int32, (LANES, wide), 1) // (2 * plan.no)
        step = plan.t * plan.a
        for w in range(plan.W):
            want = (mode // plan.kz) * MZ + w * plan.kz + mode % plan.kz
            pick = jnp.where(lane_in == want, 1.0, 0.0).astype(jnp.bfloat16)
            spread = dot16(high, pick) + dot16(low, pick)
            for k in range(2):
                rows = 0.0
                for j in range(6):
                    at = k * 6 + j
                    rows = rows + coef[at : at + 1, :] * spread[j * step : (j + 1) * step]
                rows_out[w, k] = rows

    at = pl.multiple_of(a * plan.no, plan.no)
    for w in range(plan.W):
        parts = []
        for t in range(plan.t):
            block = weights[
                0, t * plan.ky : (t + 1) * plan.ky, w * plan.kz : (w + 1) * plan.kz
            ].reshape(wide, C)
            high, low = halves(mode_block(plan, rows_out, w, t, a))
            weight, rest = halves(block)
            both = dot16(jnp.concatenate([high, low], axis=0), weight)
            parts.append(both[: 2 * n] + both[2 * n :] + dot16(high, rest))
        mixed = jnp.concatenate(parts, axis=0).T
        for g in range(plan.G):
            hold[g * plan.W + w, pl.ds(at, plan.no), :] = mixed[g * plan.no : (g + 1) * plan.no]

    @pl.when(a == plan.a - 1)
    def _():
        out[...] = hold[...].astype(jnp.bfloat16)


def inverse_kernel(plan, received, m, ex, *refs):
    out, hold = refs[-2:]
    rows = []
    for p in range(plan.PY):
        cols = []
        for q in range(plan.PZ):
            total = 0.0
            for g in range(plan.G):
                total = total + received[g * plan.W + p * plan.PZ + q].astype(jnp.float32)
            cols.append(total)
        rows.append(jnp.concatenate(cols, axis=1))
    modes = jnp.concatenate(rows, axis=0)
    nt = ((1,), (1,))
    value = dot3((m[0], m[1]), halves(modes), nt)
    size = plan.D * 8
    value = jnp.concatenate([value[:size], value[size:]], axis=1)
    value = dot3(halves(value), (ex[0], ex[1]))
    for q in range(plan.Q):
        hold[:, q * 8 : (q + 1) * 8, :] = value[:, q * LANES : (q + 1) * LANES].reshape(
            plan.D, 8, LANES
        )
    out[...] = hold[...].astype(jnp.bfloat16)


def point_kernel(plan, received, before_ref, gap_ref, zi, zf, mixc, projc, out, taken, hold):
    W, G, no = plan.W, plan.G, plan.no
    per = LANES // no
    taken[...] = received[...].astype(jnp.float32)
    tn, nt = ((0,), (0,)), ((1,), (1,))
    moments = [[0.0] * 3 for _ in range(G)]
    loss = 0.0
    for q in range(plan.Q):
        here = min(per, plan.X - q * per)
        x = slice(q * per, q * per + here)
        before = [before_ref[i, x] for i in range(3)]
        gap = [gap_ref[i, x] for i in range(3)]
        pres, gates = [], []
        shown = [0.0] * 3
        for g in range(G):
            modes = taken[g * W : (g + 1) * W, q * 8 : (q + 1) * 8, :].reshape(W * 8, LANES)
            modes = jnp.concatenate([modes, modes], axis=0)
            pre = dot16(modes, zi[...], tn)[: here * no].reshape(here, no, LANES)
            for i in range(3):
                pre = pre + mixc[g * 3 + i] * before[i]
            gate = jax.nn.sigmoid(pre)
            hidden = pre * gate
            for i in range(3):
                shown[i] = shown[i] + jnp.sum(projc[g * 3 + i] * hidden, axis=1, keepdims=True)
            pres.append(pre)
            gates.append(gate)
        residual = [shown[i] + gap[i] for i in range(3)]
        loss = loss + sum(jnp.sum(r * r, axis=0) for r in residual)
        for g in range(G):
            slope = sum(projc[g * 3 + i] * residual[i] for i in range(3))
            slope = slope * gates[g] * (1.0 + pres[g] * (1.0 - gates[g]))
            for i in range(3):
                moments[g][i] = moments[g][i] + jnp.sum(slope * before[i], axis=0)
            slope = slope.reshape(here * no, LANES)
            if here < per:
                rest = jnp.zeros(((per - here) * no, LANES), jnp.float32)
                slope = jnp.concatenate([slope, rest], axis=0)
            high, low = halves(slope)
            modes = dot16(zf[...], high, nt)
            modes = modes[: W * 8] + modes[W * 8 :] + dot16(zf[: W * 8], low, nt)
            hold[g * W : (g + 1) * W, q * 8 : (q + 1) * 8, :] = modes.reshape(W, 8, LANES)
    lanes = lane_ids(no)
    tile = jnp.zeros((no, LANES), jnp.float32)

    def place(tile, value, index):
        high = value.astype(jnp.bfloat16).astype(jnp.float32)
        tile = jnp.where(lanes == index, high, tile)
        return jnp.where(lanes == index + LANES // 2, value - high, tile)

    for g in range(G):
        for i in range(3):
            tile = place(tile, jnp.sum(moments[g][i], axis=1, keepdims=True), g * 3 + i)
    tile = place(tile, jnp.broadcast_to(jnp.sum(loss, axis=1, keepdims=True), (no, 1)), G * 3)
    hold[:, plan.Q * 8 :, :] = jnp.broadcast_to(tile[None], (plan.D, no, LANES))
    out[...] = hold[...].astype(jnp.bfloat16)


def forward_kernel(plan, received, fx, n, out, stats, taken):
    taken[...] = received[...].astype(jnp.float32)
    stats[...] = jnp.sum(taken[:, plan.Q * 8 :, :], axis=0)
    value = 0.0
    nt = ((1,), (1,))
    for q in range(plan.Q):
        rows = taken[:, q * 8 : (q + 1) * 8, :].reshape(plan.D * 8, LANES)
        cols = slice(q * LANES, (q + 1) * LANES)
        for k in range(2):
            value = value + dot16(fx[k, :, cols], rows, nt)
    size = MX * plan.no
    value = jnp.concatenate([value[:size], value[size:]], axis=1)
    modes = dot3(halves(value), (n[0], n[1])).astype(jnp.bfloat16)
    size = plan.a * plan.no
    for p in range(plan.PY):
        for q in range(plan.PZ):
            tile = modes[p * size : (p + 1) * size, q * LANES : (q + 1) * LANES]
            for g in range(plan.G):
                out[g * plan.W + p * plan.PZ + q] = tile


def grad_kernel(plan, rows_ref, received, out, taken):
    a = pl.program_id(0)
    n = plan.ky * plan.kz

    @pl.when(a == 0)
    def _():
        taken[...] = received[...].astype(jnp.float32)

    at = pl.multiple_of(a * plan.no, plan.no)
    for w in range(plan.W):
        back = jnp.concatenate(
            [taken[g * plan.W + w, pl.ds(at, plan.no), :] for g in range(plan.G)], axis=0
        ).T
        for t in range(plan.t):
            block = dot16(
                mode_block(plan, rows_ref, w, t, a), back[t * 2 * n : (t + 1) * 2 * n], ((0,), (0,))
            )
            out[0, t * plan.ky : (t + 1) * plan.ky, w * plan.kz : (w + 1) * plan.kz] = (
                block.reshape(plan.ky, plan.kz, 2, plan.no, C)
            )


def halos(faces, plan):
    xlo, xhi, ylo, yhi, zface = faces
    out = []
    for low, high, axis, count in (
        (xlo, xhi, "grp", plan.G - 1),
        (ylo, yhi, "py", plan.PY),
    ):
        up = [(i, i + 1) for i in range(count - 1)]
        out.append(lax.ppermute(high, axis, up))
        out.append(lax.ppermute(low, axis, [(j, i) for i, j in up]))
    out.append(lax.ppermute(zface, "pz", [(0, 1), (1, 0)]))
    return out


def everyone(plan, velocity, spectral_weight, lift_weight, mixing_weight, project_weight):
    tables = plan.tables()
    G, W, D = plan.G, plan.W, plan.D
    n = plan.ny
    group = lax.axis_index("grp")
    place = jnp.stack([(group == G - 1).astype(jnp.int32), lax.axis_index("pz")])
    cells = 3 * plan.nx * n
    field = velocity.reshape(cells, LANES)
    faces_shape = [shape_of(3 * n, LANES)] * 2 + [shape_of(3 * plan.nx, LANES)] * 2
    faces_shape = faces_shape + [shape_of(3 * n, LANES)]
    full = shape_of(cells, LANES)
    smem = pl.BlockSpec(memory_space=pltpu.SMEM)
    vmem = pl.BlockSpec(memory_space=pltpu.VMEM)
    hbm = pl.BlockSpec(memory_space=pl.ANY)

    def bind(kernel, *args):
        return lambda *refs: kernel(plan, *args, *refs)

    coarse_shape = (plan.cy, 3 * plan.pad, LANES)
    coarse, *faces = call(
        bind(opening_kernel),
        [shape_of(*coarse_shape)] + faces_shape,
        in_specs=[smem, vmem, vmem],
    )(place, field, tables["pairs"])
    edges = halos(faces, plan)
    coarse = lax.all_to_all(coarse, ("grp", "pz"), 0, 0, tiled=True)
    cy = lax.dynamic_index_in_dim(jnp.asarray(tables["cy"]), lax.axis_index("pz"), 0, False)
    spectra_sent = call(bind(spectrum_kernel), shape_of(D, 2 * plan.a, LANES))(
        coarse, tables["xm"], tables["tz"]
    )
    spectra = lax.all_to_all(spectra_sent, ALL, 0, 0, tiled=True)
    lines = 6 * plan.t * plan.a

    def advance(keep, share, current, edges, after):
        return call(
            bind(stage_kernel, keep, share, False),
            [full] + faces_shape,
            in_specs=[smem, hbm] + [vmem] * 7,
        )(place, after, current, field, *edges)

    one, *faces = advance(0.0, 1.0, field, edges, spectra_sent)
    edges = halos(faces, plan)

    lift = lax.dynamic_slice_in_dim(lift_weight, group * plan.no, plan.no, axis=1)
    zero = jnp.zeros_like(lift)
    first = jnp.concatenate([lift, zero], axis=1)
    second = jnp.concatenate([zero, lift], axis=1)
    coef = jnp.stack(
        [jnp.stack([first, -second], 1), jnp.stack([second, first], 1)]
    ).reshape(12, 2 * plan.no)
    wide = plan.ky * plan.kz * 2 * plan.no
    coef = jnp.tile(coef, (1, plan.ky * plan.kz))
    lift_rows, mixed = pl.pallas_call(
        bind(mix_kernel),
        grid=(plan.a,),
        in_specs=[
            pl.BlockSpec((D, 2 * plan.a, LANES), lambda i: (0, 0, 0)),
            pl.BlockSpec((2, plan.t * D, LANES), lambda i: (0, 0, 0)),
            pl.BlockSpec((12, wide), lambda i: (0, 0)),
            pl.BlockSpec((1, plan.b, MZ, 2, plan.no, C), lambda i: (i, 0, 0, 0, 0, 0)),
        ]
        + [hbm] * 5,
        out_specs=[
            pl.BlockSpec((W, 2, plan.t * plan.a, wide), lambda i: (0, 0, 0, 0)),
            pl.BlockSpec((D, plan.a * plan.no, LANES), lambda i: (0, 0, 0)),
        ],
        out_shape=[
            shape_of(W, 2, plan.t * plan.a, wide),
            shape_of(D, plan.a * plan.no, LANES, kind=jnp.bfloat16),
        ],
        scratch_shapes=[
            pltpu.VMEM((D, plan.a * plan.no, LANES), jnp.float32),
            pltpu.VMEM((lines, LANES), jnp.float32),
        ],
        compiler_params=pltpu.CompilerParams(vmem_limit_bytes=VMEM),
    )(spectra, cy, coef, spectral_weight, *edges)
    mixed_sent = mixed
    two, *faces = advance(0.75, 0.25, one, edges, mixed_sent)
    edges = halos(faces, plan)
    mixed = lax.all_to_all(mixed, ALL, 0, 0, tiled=True)

    tall = plan.Q * 8
    inner = call(
        bind(inverse_kernel),
        shape_of(D, tall, LANES, kind=jnp.bfloat16),
        [pltpu.VMEM((D, tall, LANES), jnp.float32)],
        in_specs=[vmem] * 3 + [hbm] * 5,
    )(mixed, tables["m"], tables["ex"], *edges)
    inner_sent = inner
    inner = lax.all_to_all(inner, ALL, 0, 0, tiled=True)

    three, gap = call(
        bind(stage_kernel, 1.0 / 3.0, 2.0 / 3.0, True),
        [full, shape_of(*coarse_shape, kind=jnp.bfloat16)],
        [pltpu.VMEM(coarse_shape, jnp.float32)],
        in_specs=[smem, hbm] + [vmem] * 8,
    )(place, inner_sent, two, field, *edges, tables["pairs"])
    velocity_next = three.reshape(velocity.shape)
    gap = lax.all_to_all(gap, ("grp", "pz"), 0, 0, tiled=True)

    def rows_of(value):
        value = value.reshape(G, plan.PZ, 3, plan.pad, 2, plan.cz)[: G - 1, :, :, : plan.half]
        value = value.astype(jnp.float32).transpose(2, 0, 3, 4, 1, 5)
        return value.reshape(3, plan.X, 1, plan.Z)

    def column(value):
        return value.reshape(3, G, plan.no).transpose(1, 0, 2).reshape(G * 3, plan.no, 1)

    mixc = column(contract("ic,co->io", lift_weight, mixing_weight))
    projc = column(project_weight.T)
    back = call(
        bind(point_kernel),
        shape_of(D, tall + 8, LANES, kind=jnp.bfloat16),
        [pltpu.VMEM((D, tall, LANES), jnp.float32), pltpu.VMEM((D, tall + 8, LANES), jnp.float32)],
    )(inner, rows_of(coarse), rows_of(gap), tables["zi"], tables["zf"], mixc, projc)
    back = lax.all_to_all(back, ALL, 0, 0, tiled=True)

    modes, stats = call(
        bind(forward_kernel),
        [shape_of(D, plan.a * plan.no, LANES, kind=jnp.bfloat16), shape_of(plan.no, LANES)],
        [pltpu.VMEM((D, tall + 8, LANES), jnp.float32)],
    )(back, tables["fx"], tables["n"])
    modes = lax.all_to_all(modes, ALL, 0, 0, tiled=True)

    grad_spectral = pl.pallas_call(
        bind(grad_kernel),
        grid=(plan.a,),
        in_specs=[
            pl.BlockSpec((W, 2, plan.t * plan.a, wide), lambda i: (0, 0, 0, 0)),
            pl.BlockSpec((D, plan.a * plan.no, LANES), lambda i: (0, 0, 0)),
        ],
        out_specs=pl.BlockSpec((1, plan.b, MZ, 2, plan.no, C), lambda i: (i, 0, 0, 0, 0, 0)),
        out_shape=shape_of(*spectral_weight.shape),
        scratch_shapes=[pltpu.VMEM((D, plan.a * plan.no, LANES), jnp.float32)],
        compiler_params=pltpu.CompilerParams(vmem_limit_bytes=VMEM),
    )(lift_rows, modes)

    half = LANES // 2
    stats = (stats[:, :half] + stats[:, half:]) / plan.count
    moments = stats[:, : G * 3].reshape(plan.no, G, 3).transpose(2, 1, 0).reshape(3, C)
    grad_mixing = contract("ic,io->co", lift_weight, moments)
    return velocity_next, grad_spectral, grad_mixing, 0.5 * stats[0, G * 3]


def plan_of(mesh, velocity):
    groups, rows, cols = (mesh.shape[name] for name in ALL)
    plan = Plan(groups, rows, cols, velocity.shape[1:])
    fits = (
        plan.nz == LANES
        and plan.Z == LANES
        and plan.W * plan.kz == MZ
        and plan.kz * 2 == 8
        and plan.no == 8
        and plan.ky * MZ == LANES
        and plan.t * plan.ky == plan.b
        and plan.t * 2 * plan.ky * plan.kz == LANES
        and plan.cy == groups * cols
        and plan.cx % 8 == 0
        and cols == 2
        and 2 * plan.cz == LANES
        and plan.a % 8 == 0
    )
    return plan if fits else None


def solution(mesh):
    def local(velocity, *weights):
        plan = plan_of(mesh, velocity)
        if plan is None:
            return general(velocity, *weights)
        return everyone(plan, velocity, *weights)

    return jax.shard_map(
        local,
        mesh=mesh,
        in_specs=(
            P(None, "grp", "py", "pz"),
            P("py", "pz", None, None, "grp", None),
            P(),
            P(),
            P(),
        ),
        out_specs=(P(None, "grp", "py", "pz"), P("py", "pz", None, None, "grp", None), P(), P()),
        check_vma=False,
    )
```
